256 devices in a mesh: grp: 8 (over y, core), sub: 32 (over z, x).
Axes of the slice: x: 4, y: 4, z: 8, core: 2. Of those that a mesh axis runs over, the one named last changes fastest.
Arguments:
- schur_block: float32 [8, 32, 1152, 1152], P('grp', 'sub')
- dirichlet_inverse: float32 [8, 32, 1152, 1152], P('grp', 'sub')
- coarse_basis: float32 [8, 32, 24, 1152], P('grp', 'sub'), may hold values from -0.3125 to 0.3125
- coarse_inverse: float32 [8, 768, 768], P('grp', None, 'sub')
- coarse_owner: int32 [8, 768], P('grp', 'sub'), may hold values from 0 to 767, each once within a row
- face_count: int32 [8, 32, 4], P('grp', 'sub'), may hold values from 0 to 384, as said below
- face_rows: int32 [8, 32, 4, 384], P('grp', 'sub'), may hold values from 0 to 1151, as said below
- multiplicity: int32 [8, 32, 1152], P('grp', 'sub'), may hold values from 1 to 5, as said below
- gradient: float32 [8, 32, 192, 1152], P('grp', 'sub'), may hold values from -6 to 6
- warm_start: float32 [8, 32, 192, 1152], P('grp', 'sub'), may hold values from -3 to 3
Outputs:
- adjoint: float32 [8, 32, 192, 1152], P('grp', 'sub')
The draws below stay inside these ranges and needn't reach their ends.
Inputs may be any that keep to these rules, and one draw needn't show every extreme that they name: `coarse_owner`: each group's row names each coarse unknown once. `face_count`: faces across one grp or sub step have equal counts on both sides; faces 2 and 3 at the ends of sub have count 0; some face has count 384 in every draw. `face_rows`: the live entries of one face are distinct rows; entry k of a face and entry k of the matching face of the neighbour name the same unknown; a row may lie on several faces. `multiplicity`: one plus the number of live face entries that name the row.
All inputs are finite; a program needn't handle non-finite values.
Results may differ from the reference program's by a relative error of at most 0.00023.
Values sent between devices are 32-bit elements; how exact they have to be, the bound alone decides.
A program may use at most 128 MiB of HBM per device.

```python
import jax
import jax.numpy as jnp
from jax import lax

NI = 1152
FMAX = 384
NCL = 24
RHS = 192
ITERS = 3
GROUPS = 8
SUBS = 32
CG = 768


def face_tables(key):
    base = jax.random.fold_in(key, 7001)
    key_around, key_along, key_rows = jax.random.split(base, 3)
    beside_all = jax.random.randint(key_around, (GROUPS, SUBS), FMAX // 4, FMAX + 1).astype(jnp.int32)
    beside_all = beside_all.at[0, 0].set(FMAX)
    along = jax.random.randint(key_along, (GROUPS, SUBS), FMAX // 4, FMAX + 1).astype(jnp.int32)
    along = along.at[0, 0].set(FMAX)
    along = along.at[:, SUBS - 1].set(0)
    counts = jnp.stack([beside_all, jnp.roll(beside_all, 1, axis=0), along, jnp.concatenate([jnp.zeros((GROUPS, 1), jnp.int32), along[:, :SUBS - 1]], axis=1)], axis=2)
    row_keys = jax.random.split(key_rows, GROUPS * SUBS * 4)
    chosen = jax.vmap(lambda one_key: jax.random.permutation(one_key, NI)[:FMAX])(row_keys)
    chosen = chosen.astype(jnp.int32).reshape(GROUPS, SUBS, 4, FMAX)
    live = (jnp.arange(FMAX)[None, None, None, :] < counts[..., None]).astype(jnp.int32)
    copies = jax.vmap(lambda index, mask: jnp.zeros((NI,), jnp.int32).at[index].add(mask))(chosen.reshape(GROUPS * SUBS, 4 * FMAX), live.reshape(GROUPS * SUBS, 4 * FMAX))
    return (counts, chosen, 1 + copies.reshape(GROUPS, SUBS, NI))


def dominant(key, shape, order, diag_value, spread):
    noise = jax.random.truncated_normal(key, -4.0, 4.0, shape, jnp.float32)
    return diag_value * jnp.eye(order, dtype=jnp.float32) + spread / order ** 0.5 * noise


def draw_face_count(key, part):
    return face_tables(key)[0]


def draw_face_rows(key, part):
    return face_tables(key)[1]


def draw_multiplicity(key, part):
    return face_tables(key)[2]


def draw_schur_block(key, part):
    return dominant(jax.random.fold_in(key, 11), (GROUPS, SUBS, NI, NI), NI, 2.0, 0.5)


def draw_dirichlet_inverse(key, part):
    return dominant(jax.random.fold_in(key, 13), (GROUPS, SUBS, NI, NI), NI, 0.5, 0.12)


def draw_coarse_inverse(key, part):
    return dominant(jax.random.fold_in(key, 17), (GROUPS, CG, CG), CG, 0.5, 0.15)


def steps_of(stream_key, shape, cuts, low, top_value):
    factor_of, own = 1.0, jax.random.fold_in(stream_key, 6)
    for axis_at, parts in cuts:
        draws = jnp.exp(jax.random.uniform(jax.random.fold_in(own, axis_at), (parts,), jnp.float32, low / len(cuts), top_value / len(cuts)))
        factor_of = factor_of * jnp.repeat(draws, shape[axis_at] // parts).reshape([-1 if axis == axis_at else 1 for axis in range(len(shape))])
    return factor_of


def gaussian(key, shape, deviation, limit, cuts=(), held_as=jnp.bfloat16):
    entries = jax.random.normal(key, shape, jnp.float32) * deviation
    if len(cuts) > 0:
        entries = steps_of(key, shape, cuts, -0.22, 0.18) * entries
    return jnp.clip(entries, min=-limit, max=limit).astype(held_as)


def setup_inputs(seed: int = 0) -> dict:
    arg_keys = jax.random.split(jax.random.key(seed), 11)
    schur_block = draw_schur_block(jax.random.fold_in(arg_keys[10], 71), 0)
    dirichlet_inverse = draw_dirichlet_inverse(jax.random.fold_in(arg_keys[10], 71), 0)
    coarse_basis = gaussian(arg_keys[2], (GROUPS, SUBS, NCL, NI), (NI // 3) ** -0.5, 0.3125, ((0, 8), (1, 32)), jnp.float32)
    coarse_inverse = draw_coarse_inverse(jax.random.fold_in(arg_keys[10], 71), 0)
    coarse_owner = jax.vmap(lambda own: jax.random.permutation(own, CG))(jax.random.split(arg_keys[4], GROUPS)).reshape((GROUPS, CG)).astype(jnp.int32)
    face_count = draw_face_count(jax.random.fold_in(arg_keys[10], 71), 0)
    face_rows = draw_face_rows(jax.random.fold_in(arg_keys[10], 71), 0)
    multiplicity = draw_multiplicity(jax.random.fold_in(arg_keys[10], 71), 0)
    gradient = gaussian(arg_keys[8], (GROUPS, SUBS, RHS, NI), 1.0, 6.0, ((0, 8), (1, 32)), jnp.float32)
    warm_start = gaussian(arg_keys[9], (GROUPS, SUBS, RHS, NI), 0.5, 3.0, ((0, 8), (1, 32)), jnp.float32)
    return dict(schur_block=schur_block, dirichlet_inverse=dirichlet_inverse, coarse_basis=coarse_basis, coarse_inverse=coarse_inverse, coarse_owner=coarse_owner, face_count=face_count, face_rows=face_rows, multiplicity=multiplicity, gradient=gradient, warm_start=warm_start)


HIGHEST = lax.Precision.HIGHEST


def face_sum(values, face_rows, live_mask):
    def pick(block, index, mask):
        return jax.vmap(lambda one_index, one_mask: block[:, one_index] * one_mask[None, :])(index, mask)

    outgoing = jax.vmap(jax.vmap(pick))(values, face_rows, live_mask)
    zero_edge = jnp.zeros_like(outgoing[:, :1, 0])
    incoming = jnp.stack([
        jnp.roll(outgoing[:, :, 1], -1, axis=0),
        jnp.roll(outgoing[:, :, 0], 1, axis=0),
        jnp.concatenate([outgoing[:, 1:, 3], zero_edge], axis=1),
        jnp.concatenate([zero_edge, outgoing[:, :-1, 2]], axis=1)], axis=2)

    def place(block, index, arriving):
        for face in range(4):
            block = block.at[:, index[face]].add(arriving[face])
        return block

    return jax.vmap(jax.vmap(place))(values, face_rows, incoming)


def reference(schur_block, dirichlet_inverse, coarse_basis, coarse_inverse, coarse_owner, face_count, face_rows, multiplicity, gradient, warm_start):
    live_mask = (jnp.arange(FMAX)[None, None, None, :] < face_count[..., None]).astype(jnp.float32)
    weight = (1.0 / multiplicity.astype(jnp.float32))[:, :, None, :]
    owner_slots = coarse_owner.reshape(GROUPS, SUBS, NCL)
    adjoint = warm_start
    for iteration in range(ITERS):
        applied = jnp.einsum('gsri,gsik->gsrk', adjoint, schur_block, precision=HIGHEST)
        residual = gradient - face_sum(applied, face_rows, live_mask)
        weighted = weight * residual
        local_part = jnp.einsum('gsri,gsik->gsrk', weighted, dirichlet_inverse, precision=HIGHEST)
        coarse_piece = jnp.einsum('gsri,gsji->gsrj', weighted, coarse_basis, precision=HIGHEST)
        slots = jnp.transpose(coarse_piece, (0, 2, 1, 3)).reshape(GROUPS, RHS, CG)
        coarse_sum = jax.vmap(lambda placed, owner: jnp.zeros((RHS, CG), jnp.float32).at[:, owner].set(placed))(slots, coarse_owner)
        coarse_solution = jnp.einsum('grj,gjk->grk', coarse_sum, coarse_inverse, precision=HIGHEST)
        picked = jax.vmap(lambda solution, owner: solution[:, owner])(coarse_solution, owner_slots)
        correction = jnp.einsum('grsj,gsji->gsri', picked, coarse_basis, precision=HIGHEST)
        adjoint = adjoint + face_sum(weight * (local_part + correction), face_rows, live_mask)
    return adjoint
```

```python
import functools

import jax
import jax.numpy as jnp
from jax import lax
from jax.experimental import pallas as pl
from jax.experimental.pallas import tpu as pltpu
from jax.sharding import PartitionSpec as P

ITERS = 3
NI = 1152
FMAX = 384
NCL = 24
RHS = 192
GROUPS = 8
SUBS = 32
CG = 768
BF = jnp.bfloat16
F32 = jnp.float32
HIGHEST = lax.Precision.HIGHEST
MESH = pl.DeviceIdType.MESH
NN = (((1,), (0,)), ((), ()))
NT = (((1,), (1,)), ((), ()))
TN = (((0,), (0,)), ((), ()))


def parts(value):
    high = value.astype(BF)
    return high, (value - high.astype(F32)).astype(BF)


def dot(left, right, dims=NN):
    return lax.dot_general(left, right, dims, preferred_element_type=F32)


def three(left, right, dims):
    left_high, left_low = parts(left)
    right_high, right_low = parts(right)
    return (
        dot(left_high, right_high, dims)
        + dot(left_low, right_high, dims)
        + dot(left_high, right_low, dims)
    )


def kernel(
    schur_high, schur_low, dirichlet_high, dirichlet_low, basis, mixing, pick, place, weight,
    gradient, warm, out,
    adjoint, values, stacked, send, recv, pieces, face_sent, face_got, piece_sent, piece_got,
):
    grp = lax.axis_index("grp")
    sub = lax.axis_index("sub")
    around = (lax.rem(grp + 1, GROUPS), lax.rem(grp + GROUPS - 1, GROUPS))
    along = (lax.rem(sub + 1, SUBS), lax.rem(sub + SUBS - 1, SUBS))
    targets = (
        (around[0], sub),
        (around[1], sub),
        (grp, along[0]),
        (grp, along[1]),
    )

    barrier = pltpu.get_barrier_semaphore()
    for target in targets[:2]:
        pl.semaphore_signal(barrier, inc=1, device_id=target, device_id_type=MESH)

    def greet(step, carry):
        pl.semaphore_signal(
            barrier, inc=1, device_id=(grp, lax.rem(sub + step, SUBS)), device_id_type=MESH
        )
        return carry

    lax.fori_loop(1, SUBS, greet, 0)
    pl.semaphore_wait(barrier, SUBS + 1)

    def stack(value):
        rows = value.shape[0]
        high, low = parts(value)
        return jnp.concatenate([high, low], axis=0)

    def product(source, high, low):
        stacked[...] = stack(source)
        for start, size in ((0, 512), (512, 640)):
            both = dot(stacked[...], high[:, start : start + size])
            values[:, start : start + size] = (
                both[:RHS] + both[RHS:] + dot(stacked[:RHS], low[:, start : start + size])
            )

    def face_copy(phase, face):
        return pltpu.make_async_remote_copy(
            src_ref=send.at[face],
            dst_ref=recv.at[phase, face ^ 1],
            send_sem=face_sent.at[phase, face],
            recv_sem=face_got.at[phase, face ^ 1],
            device_id=targets[face],
            device_id_type=MESH,
        )

    def assemble(phase):
        stacked[...] = stack(values[...])
        for pair in (1, 0):
            both = dot(stacked[...], pick[pair])
            chosen = both[:RHS] + both[RHS:]
            for side in (0, 1):
                send[2 * pair + side] = chosen[:, side * FMAX : (side + 1) * FMAX]
                face_copy(phase, 2 * pair + side).start()
        for pair in (0, 1):
            for side in (0, 1):
                pltpu.make_async_remote_copy(
                    src_ref=send.at[2 * pair + side],
                    dst_ref=recv.at[phase, 2 * pair + side],
                    send_sem=face_sent.at[phase, 2 * pair + side],
                    recv_sem=face_got.at[phase, 2 * pair + side],
                    device_id=targets[2 * pair + side],
                    device_id_type=MESH,
                ).wait_recv()
            arrived = stack(
                jnp.concatenate([recv[phase, 2 * pair], recv[phase, 2 * pair + 1]], axis=1)
            )
            both = dot(arrived, place[pair])
            values[...] += both[:RHS] + both[RHS:]
        for face in range(4):
            face_copy(phase, face).wait_send()

    adjoint[...] = warm[...]

    def iterate(iteration, carry):
        product(adjoint[...], schur_high, schur_low)
        assemble(2 * iteration)
        weighted = (gradient[...] - values[...]) * weight[...]
        pieces[iteration, sub] = three(basis[...], weighted, NT)

        def piece_copy(step, landing):
            return pltpu.make_async_remote_copy(
                src_ref=pieces.at[iteration, sub],
                dst_ref=pieces.at[iteration, landing],
                send_sem=piece_sent.at[iteration, step],
                recv_sem=piece_got.at[iteration, step],
                device_id=(grp, lax.rem(sub + step, SUBS)),
                device_id_type=MESH,
            )

        def launch(step, carry):
            piece_copy(step, sub).start()
            return carry

        lax.fori_loop(1, SUBS, launch, 0)
        product(weighted, dirichlet_high, dirichlet_low)

        def land(step, carry):
            piece_copy(step, lax.rem(sub + SUBS - step, SUBS)).wait_recv()
            return carry

        lax.fori_loop(1, SUBS, land, 0)
        gathered = pieces[iteration].reshape(CG, RHS)
        picked = three(mixing[...], gathered, NN)
        values[...] = (values[...] + three(picked, basis[...], TN)) * weight[...]
        assemble(2 * iteration + 1)
        adjoint[...] += values[...]

        def leave(step, carry):
            piece_copy(step, sub).wait_send()
            return carry

        lax.fori_loop(1, SUBS, leave, 0)
        return carry

    lax.fori_loop(0, ITERS, iterate, 0)
    out[...] = adjoint[...]


def split(matrix):
    high = lax.reduce_precision(matrix, 8, 7)
    return high.astype(BF), (matrix - high).astype(BF)


def local(
    schur_block,
    dirichlet_inverse,
    coarse_basis,
    coarse_inverse,
    coarse_owner,
    face_count,
    face_rows,
    multiplicity,
    gradient,
    warm_start,
):
    my_owner = coarse_owner[0]
    all_owner = lax.all_gather(coarse_owner, "sub", axis=1, tiled=True)[0]
    inverse_columns = lax.all_gather(coarse_inverse[0].T, "sub", axis=0, tiled=True)
    order = (jnp.arange(CG)[:, None] == all_owner[None, :]).astype(F32)
    mixing = jnp.dot(inverse_columns[my_owner], order, precision=HIGHEST, preferred_element_type=F32)

    face_index = face_rows[0, 0]
    live = jnp.arange(FMAX)[None, :] < face_count[0, 0][:, None]
    masked = jnp.where(live, face_index, NI).reshape(2, 2 * FMAX)
    rows = jnp.arange(NI)
    pick = (rows[None, :, None] == masked[:, None, :]).astype(BF)
    place = (masked[:, :, None] == rows[None, None, :]).astype(BF)
    weight = (1.0 / multiplicity[0, 0].astype(F32))[None, :]
    schur_high, schur_low = split(schur_block[0, 0])
    dirichlet_high, dirichlet_low = split(dirichlet_inverse[0, 0])

    vmem = pl.BlockSpec(memory_space=pltpu.VMEM)
    out = pl.pallas_call(
        kernel,
        out_shape=jax.ShapeDtypeStruct((RHS, NI), F32),
        in_specs=[vmem] * 11,
        out_specs=vmem,
        scratch_shapes=[
            pltpu.VMEM((RHS, NI), F32),
            pltpu.VMEM((RHS, NI), F32),
            pltpu.VMEM((2 * RHS, NI), BF),
            pltpu.VMEM((4, RHS, FMAX), F32),
            pltpu.VMEM((2 * ITERS, 4, RHS, FMAX), F32),
            pltpu.VMEM((ITERS, SUBS, NCL, RHS), F32),
            pltpu.SemaphoreType.DMA((2 * ITERS, 4)),
            pltpu.SemaphoreType.DMA((2 * ITERS, 4)),
            pltpu.SemaphoreType.DMA((ITERS, SUBS)),
            pltpu.SemaphoreType.DMA((ITERS, SUBS)),
        ],
        compiler_params=pltpu.CompilerParams(
            collective_id=0, has_side_effects=True, vmem_limit_bytes=60 * 1024 * 1024
        ),
    )(
        schur_high, schur_low, dirichlet_high, dirichlet_low, coarse_basis[0, 0], mixing, pick, place,
        weight, gradient[0, 0], warm_start[0, 0],
    )
    return out[None, None]


def solution(mesh):
    in_specs = (
        P("grp", "sub", None, None),
        P("grp", "sub", None, None),
        P("grp", "sub", None, None),
        P("grp", None, "sub"),
        P("grp", "sub"),
        P("grp", "sub", None),
        P("grp", "sub", None, None),
        P("grp", "sub", None),
        P("grp", "sub", None, None),
        P("grp", "sub", None, None),
    )
    out_specs = P("grp", "sub", None, None)
    return jax.shard_map(local, mesh=mesh, in_specs=in_specs, out_specs=out_specs, check_vma=False)
```

```python
import functools

import jax
import jax.numpy as jnp
from jax import lax
from jax.experimental import pallas as pl
from jax.experimental.pallas import tpu as pltpu
from jax.sharding import PartitionSpec as P

ITERS = 3
NI = 1152
FMAX = 384
NCL = 24
RHS = 192
GROUPS = 8
SUBS = 32
CG = 768
BF = jnp.bfloat16
F32 = jnp.float32
HIGHEST = lax.Precision.HIGHEST
MESH = pl.DeviceIdType.MESH
NN = (((1,), (0,)), ((), ()))
NT = (((1,), (1,)), ((), ()))
TN = (((0,), (0,)), ((), ()))


def parts(value):
    high = value.astype(BF)
    return high, (value - high.astype(F32)).astype(BF)


def dot(left, right, dims=NN):
    return lax.dot_general(left, right, dims, preferred_element_type=F32)


def three(left, right, dims):
    left_high, left_low = parts(left)
    right_high, right_low = parts(right)
    return (
        dot(left_high, right_high, dims)
        + dot(left_low, right_high, dims)
        + dot(left_high, right_low, dims)
    )


def kernel(
    schur, dirichlet, basis, inverse_block, my_owner, row_of, column_of, weight,
    gradient, warm, adjoint,
    schur_high, schur_low, dirichlet_high, dirichlet_low, pick, place, mixing, inverse,
    values, stacked, send, recv, pieces, face_sent, face_got, piece_sent, piece_got,
    inverse_sent, inverse_got, own_sem,
):
    grp = lax.axis_index("grp")
    sub = lax.axis_index("sub")
    across = lax.rem(sub, 4)
    around = (lax.rem(grp + 1, GROUPS), lax.rem(grp + GROUPS - 1, GROUPS))
    along = (lax.rem(sub + 1, SUBS), lax.rem(sub + SUBS - 1, SUBS))
    targets = (
        (around[0], sub),
        (around[1], sub),
        (grp, along[0]),
        (grp, along[1]),
    )

    def down(step):
        return (grp, lax.rem(sub + 4 * step, SUBS))

    def aside(step):
        return (grp, sub - across + lax.rem(across + step, 4))

    barrier = pltpu.get_barrier_semaphore()
    greeted = targets + tuple(down(step) for step in range(1, 8)) + tuple(aside(step) for step in range(1, 4))
    for target in greeted:
        pl.semaphore_signal(barrier, inc=1, device_id=target, device_id_type=MESH)
    pltpu.make_async_copy(inverse_block, inverse.at[sub], own_sem).start()
    pltpu.make_async_copy(inverse_block, inverse.at[sub], own_sem).wait()
    pl.semaphore_wait(barrier, len(greeted))

    def owner_down(step):
        return lax.rem(sub + SUBS - 4 * step, SUBS)

    def owner_aside(step, over):
        start = sub - across + lax.rem(across + 4 - over, 4)
        return lax.rem(start + SUBS - 4 * step, SUBS)

    def block_copy(buffer, sent, got, source, landing, step, over, target):
        return pltpu.make_async_remote_copy(
            src_ref=buffer.at[source],
            dst_ref=buffer.at[landing],
            send_sem=sent.at[4 * step + over],
            recv_sem=got.at[4 * step + over],
            device_id=target,
            device_id_type=MESH,
        )

    def gather_start(buffer, sent, got):
        def body(step, carry):
            block_copy(buffer, sent, got, sub, sub, step, 0, down(step)).start()
            return carry

        lax.fori_loop(1, 8, body, 0)

    def relay(buffer, sent, got, step):
        owner = owner_down(step)
        for over in (1, 3, 2):
            block_copy(buffer, sent, got, owner, owner, step, over, aside(over)).start()

    def gather_relay(buffer, sent, got):
        relay(buffer, sent, got, 0)

        def body(position, carry):
            step = lax.rem(position, 2) * (8 - (position + 1) // 2) + (1 - lax.rem(position, 2)) * (position // 2)
            owner = owner_down(step)
            block_copy(buffer, sent, got, owner, owner, step, 0, down(step)).wait_recv()
            relay(buffer, sent, got, step)
            return carry

        lax.fori_loop(1, 8, body, 0)

    def gather_finish(buffer, sent, got):
        def body(step, carry):
            for over in (1, 2, 3):
                owner = owner_aside(step, over)
                block_copy(buffer, sent, got, owner, owner, step, over, aside(over)).wait_recv()
            return carry

        lax.fori_loop(0, 8, body, 0)

    def gather_leave(buffer, sent, got):
        def one(step, carry):
            block_copy(buffer, sent, got, sub, sub, step, 0, down(step)).wait_send()
            return carry

        lax.fori_loop(1, 8, one, 0)

        def body(step, carry):
            owner = owner_down(step)
            for over in (1, 2, 3):
                block_copy(buffer, sent, got, owner, owner, step, over, aside(over)).wait_send()
            return carry

        lax.fori_loop(0, 8, body, 0)

    gather_start(inverse, inverse_sent, inverse_got)

    def split(matrix, high_ref, low_ref):
        def body(step, carry):
            rows = pl.ds(pl.multiple_of(step * 128, 128), 128)
            high_ref[rows, :], low_ref[rows, :] = parts(matrix[rows, :])
            return carry

        lax.fori_loop(0, NI // 128, body, 0)

    split(schur, schur_high, schur_low)
    for pair in (0, 1):

        def pick_rows(step, carry):
            first = pl.multiple_of(step * 128, 128)
            names = first + lax.broadcasted_iota(jnp.int32, (128, 2 * FMAX), 0)
            pick[pair, pl.ds(first, 128), :] = jnp.where(names == row_of[pair], 1.0, 0.0).astype(BF)
            return carry

        lax.fori_loop(0, NI // 128, pick_rows, 0)

        def place_rows(step, carry):
            rows = pl.ds(pl.multiple_of(step * 128, 128), 128)
            names = lax.broadcasted_iota(jnp.int32, (128, NI), 1)
            place[pair, rows, :] = jnp.where(names == column_of[pair, rows, :], 1.0, 0.0).astype(BF)
            return carry

        lax.fori_loop(0, 2 * FMAX // 128, place_rows, 0)

    def stack(value):
        rows = value.shape[0]
        high, low = parts(value)
        return jnp.concatenate([high, low], axis=0)

    def product(source, high, low):
        stacked[...] = stack(source)
        for start, size in ((0, 512), (512, 640)):
            both = dot(stacked[...], high[:, start : start + size])
            values[:, start : start + size] = (
                both[:RHS] + both[RHS:] + dot(stacked[:RHS], low[:, start : start + size])
            )

    def face_copy(phase, face):
        return pltpu.make_async_remote_copy(
            src_ref=send.at[face],
            dst_ref=recv.at[phase, face ^ 1],
            send_sem=face_sent.at[phase, face],
            recv_sem=face_got.at[phase, face ^ 1],
            device_id=targets[face],
            device_id_type=MESH,
        )

    def assemble(phase, between):
        stacked[...] = stack(values[...])
        for pair in (1, 0):
            both = dot(stacked[...], pick[pair])
            chosen = both[:RHS] + both[RHS:]
            for side in (0, 1):
                send[2 * pair + side] = chosen[:, side * FMAX : (side + 1) * FMAX]
                face_copy(phase, 2 * pair + side).start()
        between()
        for pair in (0, 1):
            for side in (0, 1):
                pltpu.make_async_remote_copy(
                    src_ref=send.at[2 * pair + side],
                    dst_ref=recv.at[phase, 2 * pair + side],
                    send_sem=face_sent.at[phase, 2 * pair + side],
                    recv_sem=face_got.at[phase, 2 * pair + side],
                    device_id=targets[2 * pair + side],
                    device_id_type=MESH,
                ).wait_recv()
            arrived = stack(
                jnp.concatenate([recv[phase, 2 * pair], recv[phase, 2 * pair + 1]], axis=1)
            )
            both = dot(arrived, place[pair])
            values[...] += both[:RHS] + both[RHS:]
        for face in range(4):
            face_copy(phase, face).wait_send()

    adjoint[...] = warm[...]

    def mix():
        gather_finish(inverse, inverse_sent, inverse_got)
        everyone = inverse[...].reshape(CG, CG + 128)
        names = lax.broadcasted_iota(jnp.int32, (CG, CG), 1).astype(F32)
        order = jnp.where(names == everyone[:, CG : CG + 1], 1.0, 0.0).astype(BF)
        mine = jnp.where(
            lax.broadcasted_iota(jnp.int32, (NCL, CG), 1) == my_owner[...], 1.0, 0.0
        ).astype(BF)
        high, low = parts(everyone[:, :CG])
        columns = dot(mine, high) + dot(mine, low)
        high, low = parts(columns)
        mixing[...] = dot(high, order, NT) + dot(low, order, NT)

    def iterate(iteration, carry):
        block = (pieces.at[iteration], piece_sent.at[iteration], piece_got.at[iteration])
        product(adjoint[...], schur_high, schur_low)

        def first_wait():
            @pl.when(iteration == 0)
            def _():
                split(dirichlet, dirichlet_high, dirichlet_low)
                gather_relay(inverse, inverse_sent, inverse_got)

        assemble(2 * iteration, first_wait)
        weighted = (gradient[...] - values[...]) * weight[...]
        pieces[iteration, sub] = three(basis[...], weighted, NT)
        gather_start(*block)
        product(weighted, dirichlet_high, dirichlet_low)
        gather_relay(*block)

        @pl.when(iteration == 0)
        def _():
            mix()

        gather_finish(*block)
        gathered = pieces[iteration].reshape(CG, RHS)
        picked = three(mixing[...], gathered, NN)
        values[...] = (values[...] + three(picked, basis[...], TN)) * weight[...]
        assemble(2 * iteration + 1, lambda: gather_leave(*block))
        adjoint[...] += values[...]
        return carry

    lax.fori_loop(0, ITERS, iterate, 0)
    gather_leave(inverse, inverse_sent, inverse_got)


def local(
    schur_block,
    dirichlet_inverse,
    coarse_basis,
    coarse_inverse,
    coarse_owner,
    face_count,
    face_rows,
    multiplicity,
    gradient,
    warm_start,
):
    my_owner = coarse_owner[0][:, None]
    inverse_block = jnp.concatenate(
        [coarse_inverse[0].T, jnp.broadcast_to(my_owner.astype(F32), (NCL, 128))], axis=1
    )
    live = jnp.arange(FMAX)[None, :] < face_count[0, 0][:, None]
    masked = jnp.where(live, face_rows[0, 0], NI).reshape(2, 2 * FMAX)
    weight = (1.0 / multiplicity[0, 0].astype(F32))[None, :]

    vmem = pl.BlockSpec(memory_space=pltpu.VMEM)
    out = pl.pallas_call(
        kernel,
        out_shape=jax.ShapeDtypeStruct((RHS, NI), F32),
        in_specs=[vmem] * 10,
        out_specs=vmem,
        scratch_shapes=[
            pltpu.VMEM((NI, NI), BF),
            pltpu.VMEM((NI, NI), BF),
            pltpu.VMEM((NI, NI), BF),
            pltpu.VMEM((NI, NI), BF),
            pltpu.VMEM((2, NI, 2 * FMAX), BF),
            pltpu.VMEM((2, 2 * FMAX, NI), BF),
            pltpu.VMEM((NCL, CG), F32),
            pltpu.VMEM((SUBS, NCL, CG + 128), F32),
            pltpu.VMEM((RHS, NI), F32),
            pltpu.VMEM((2 * RHS, NI), BF),
            pltpu.VMEM((4, RHS, FMAX), F32),
            pltpu.VMEM((2 * ITERS, 4, RHS, FMAX), F32),
            pltpu.VMEM((ITERS, SUBS, NCL, RHS), F32),
            pltpu.SemaphoreType.DMA((2 * ITERS, 4)),
            pltpu.SemaphoreType.DMA((2 * ITERS, 4)),
            pltpu.SemaphoreType.DMA((ITERS, SUBS)),
            pltpu.SemaphoreType.DMA((ITERS, SUBS)),
            pltpu.SemaphoreType.DMA((SUBS,)),
            pltpu.SemaphoreType.DMA((SUBS,)),
            pltpu.SemaphoreType.DMA,
        ],
        compiler_params=pltpu.CompilerParams(
            collective_id=0, has_side_effects=True, vmem_limit_bytes=63 * 1024 * 1024
        ),
    )(
        schur_block[0, 0], dirichlet_inverse[0, 0], coarse_basis[0, 0], inverse_block, my_owner,
        masked[:, None, :], masked[:, :, None], weight, gradient[0, 0], warm_start[0, 0],
    )
    return out[None, None]


def solution(mesh):
    in_specs = (
        P("grp", "sub", None, None),
        P("grp", "sub", None, None),
        P("grp", "sub", None, None),
        P("grp", None, "sub"),
        P("grp", "sub"),
        P("grp", "sub", None),
        P("grp", "sub", None, None),
        P("grp", "sub", None),
        P("grp", "sub", None, None),
        P("grp", "sub", None, None),
    )
    out_specs = P("grp", "sub", None, None)
    return jax.shard_map(local, mesh=mesh, in_specs=in_specs, out_specs=out_specs, check_vma=False)
```

```python
import functools

import jax
import jax.numpy as jnp
from jax import lax
from jax.experimental import pallas as pl
from jax.experimental.pallas import tpu as pltpu
from jax.sharding import PartitionSpec as P

ITERS = 3
NI = 1152
FMAX = 384
NCL = 24
RHS = 192
GROUPS = 8
SUBS = 32
CG = 768
BF = jnp.bfloat16
F32 = jnp.float32
HIGHEST = lax.Precision.HIGHEST
MESH = pl.DeviceIdType.MESH
NN = (((1,), (0,)), ((), ()))
NT = (((1,), (1,)), ((), ()))
TN = (((0,), (0,)), ((), ()))


def parts(value):
    high = value.astype(BF)
    return high, (value - high.astype(F32)).astype(BF)


def dot(left, right, dims=NN):
    return lax.dot_general(left, right, dims, preferred_element_type=F32)


def three(left, right, dims):
    left_high, left_low = parts(left)
    right_high, right_low = parts(right)
    return (
        dot(left_high, right_high, dims)
        + dot(left_low, right_high, dims)
        + dot(left_high, right_low, dims)
    )


def kernel(
    schur, dirichlet, basis, inverse_block, my_owner, row_of, column_of, weight,
    gradient, warm, adjoint,
    schur_high, schur_low, dirichlet_high, dirichlet_low, pick, place, mixing, inverse,
    values, stacked, send, recv, pieces, face_sent, face_got, piece_sent, piece_got,
    inverse_sent, inverse_got, own_sem,
):
    grp = lax.axis_index("grp")
    sub = lax.axis_index("sub")
    across = lax.rem(sub, 4)
    around = (lax.rem(grp + 1, GROUPS), lax.rem(grp + GROUPS - 1, GROUPS))
    along = (lax.rem(sub + 1, SUBS), lax.rem(sub + SUBS - 1, SUBS))
    targets = (
        (around[0], sub),
        (around[1], sub),
        (grp, along[0]),
        (grp, along[1]),
    )

    def down(step):
        return (grp, lax.rem(sub + 4 * step, SUBS))

    def aside(step):
        return (grp, sub - across + lax.rem(across + step, 4))

    barrier = pltpu.get_barrier_semaphore()
    greeted = targets + tuple(down(step) for step in range(1, 8)) + tuple(aside(step) for step in range(1, 4))
    for target in greeted:
        pl.semaphore_signal(barrier, inc=1, device_id=target, device_id_type=MESH)
    pltpu.make_async_copy(inverse_block, inverse.at[sub], own_sem).start()
    pltpu.make_async_copy(inverse_block, inverse.at[sub], own_sem).wait()
    pl.semaphore_wait(barrier, len(greeted))

    def owner_down(step):
        return lax.rem(sub + SUBS - 4 * step, SUBS)

    def owner_aside(step, over):
        start = sub - across + lax.rem(across + 4 - over, 4)
        return lax.rem(start + SUBS - 4 * step, SUBS)

    def block_copy(buffer, sent, got, source, landing, step, over, target):
        return pltpu.make_async_remote_copy(
            src_ref=buffer.at[source],
            dst_ref=buffer.at[landing],
            send_sem=sent.at[4 * step + over],
            recv_sem=got.at[4 * step + over],
            device_id=target,
            device_id_type=MESH,
        )

    def gather_start(buffer, sent, got):
        def body(step, carry):
            block_copy(buffer, sent, got, sub, sub, step, 0, down(step)).start()
            return carry

        lax.fori_loop(1, 8, body, 0)

    def nearest(position):
        odd = lax.rem(position, 2)
        return odd * (8 - (position + 1) // 2) + (1 - odd) * (position // 2)

    def far_copy(buffer, sent, got, step):
        side = 1 + 2 * lax.rem(step, 2)
        owner = owner_aside(step, side)
        return block_copy(buffer, sent, got, owner, owner, step, 2, aside(side))

    def relay(buffer, sent, got, step):
        owner = owner_down(step)
        for over in (1, 3):
            block_copy(buffer, sent, got, owner, owner, step, over, aside(over)).start()

    def gather_relay(buffer, sent, got):
        relay(buffer, sent, got, 0)

        def body(position, carry):
            step = nearest(position)
            owner = owner_down(step)
            block_copy(buffer, sent, got, owner, owner, step, 0, down(step)).wait_recv()
            relay(buffer, sent, got, step)
            return carry

        lax.fori_loop(1, 8, body, 0)

    def gather_forward(buffer, sent, got):
        def body(position, carry):
            step = nearest(position)
            side = 1 + 2 * lax.rem(step, 2)
            owner = owner_aside(step, side)
            block_copy(buffer, sent, got, owner, owner, step, side, aside(side)).wait_recv()
            far_copy(buffer, sent, got, step).start()
            return carry

        lax.fori_loop(0, 8, body, 0)

    def gather_finish(buffer, sent, got):
        def body(step, carry):
            for over in (3 - 2 * lax.rem(step, 2), 2):
                owner = owner_aside(step, over)
                block_copy(buffer, sent, got, owner, owner, step, over, aside(over)).wait_recv()
            return carry

        lax.fori_loop(0, 8, body, 0)

    def gather_leave(buffer, sent, got):
        def one(step, carry):
            block_copy(buffer, sent, got, sub, sub, step, 0, down(step)).wait_send()
            return carry

        lax.fori_loop(1, 8, one, 0)

        def body(step, carry):
            owner = owner_down(step)
            for over in (1, 3):
                block_copy(buffer, sent, got, owner, owner, step, over, aside(over)).wait_send()
            far_copy(buffer, sent, got, step).wait_send()
            return carry

        lax.fori_loop(0, 8, body, 0)

    gather_start(inverse, inverse_sent, inverse_got)

    def split(matrix, high_ref, low_ref):
        def body(step, carry):
            rows = pl.ds(pl.multiple_of(step * 128, 128), 128)
            high_ref[rows, :], low_ref[rows, :] = parts(matrix[rows, :])
            return carry

        lax.fori_loop(0, NI // 128, body, 0)

    split(schur, schur_high, schur_low)
    for pair in (0, 1):

        def pick_rows(step, carry):
            first = pl.multiple_of(step * 128, 128)
            names = first + lax.broadcasted_iota(jnp.int32, (128, 2 * FMAX), 0)
            pick[pair, pl.ds(first, 128), :] = jnp.where(names == row_of[pair], 1.0, 0.0).astype(BF)
            return carry

        lax.fori_loop(0, NI // 128, pick_rows, 0)

        def place_rows(step, carry):
            rows = pl.ds(pl.multiple_of(step * 128, 128), 128)
            names = lax.broadcasted_iota(jnp.int32, (128, NI), 1)
            place[pair, rows, :] = jnp.where(names == column_of[pair, rows, :], 1.0, 0.0).astype(BF)
            return carry

        lax.fori_loop(0, 2 * FMAX // 128, place_rows, 0)

    def stack(value):
        rows = value.shape[0]
        high, low = parts(value)
        return jnp.concatenate([high, low], axis=0)

    def product(source, high, low):
        stacked[...] = stack(source)
        for start, size in ((0, 512), (512, 640)):
            both = dot(stacked[...], high[:, start : start + size])
            values[:, start : start + size] = (
                both[:RHS] + both[RHS:] + dot(stacked[:RHS], low[:, start : start + size])
            )

    def face_copy(phase, face):
        return pltpu.make_async_remote_copy(
            src_ref=send.at[face],
            dst_ref=recv.at[phase, face ^ 1],
            send_sem=face_sent.at[phase, face],
            recv_sem=face_got.at[phase, face ^ 1],
            device_id=targets[face],
            device_id_type=MESH,
        )

    def assemble(phase, between):
        stacked[...] = stack(values[...])
        for pair in (1, 0):
            both = dot(stacked[...], pick[pair])
            chosen = both[:RHS] + both[RHS:]
            for side in (0, 1):
                send[2 * pair + side] = chosen[:, side * FMAX : (side + 1) * FMAX]
                face_copy(phase, 2 * pair + side).start()
        between()
        for pair in (0, 1):
            for side in (0, 1):
                pltpu.make_async_remote_copy(
                    src_ref=send.at[2 * pair + side],
                    dst_ref=recv.at[phase, 2 * pair + side],
                    send_sem=face_sent.at[phase, 2 * pair + side],
                    recv_sem=face_got.at[phase, 2 * pair + side],
                    device_id=targets[2 * pair + side],
                    device_id_type=MESH,
                ).wait_recv()
            arrived = stack(
                jnp.concatenate([recv[phase, 2 * pair], recv[phase, 2 * pair + 1]], axis=1)
            )
            both = dot(arrived, place[pair])
            values[...] += both[:RHS] + both[RHS:]
        for face in range(4):
            face_copy(phase, face).wait_send()

    adjoint[...] = warm[...]

    def mix():
        gather_finish(inverse, inverse_sent, inverse_got)
        everyone = inverse[...].reshape(CG, CG + 128)
        names = lax.broadcasted_iota(jnp.int32, (CG, CG), 1).astype(F32)
        order = jnp.where(names == everyone[:, CG : CG + 1], 1.0, 0.0).astype(BF)
        mine = jnp.where(
            lax.broadcasted_iota(jnp.int32, (NCL, CG), 1) == my_owner[...], 1.0, 0.0
        ).astype(BF)
        high, low = parts(everyone[:, :CG])
        columns = dot(mine, high) + dot(mine, low)
        high, low = parts(columns)
        mixing[...] = dot(high, order, NT) + dot(low, order, NT)

    def iterate(iteration, carry):
        block = (pieces.at[iteration], piece_sent.at[iteration], piece_got.at[iteration])
        product(adjoint[...], schur_high, schur_low)

        def first_wait():
            @pl.when(iteration == 0)
            def _():
                split(dirichlet, dirichlet_high, dirichlet_low)
                gather_relay(inverse, inverse_sent, inverse_got)

        assemble(2 * iteration, first_wait)
        weighted = (gradient[...] - values[...]) * weight[...]
        pieces[iteration, sub] = three(basis[...], weighted, NT)
        gather_start(*block)

        @pl.when(iteration == 0)
        def _():
            gather_forward(inverse, inverse_sent, inverse_got)

        product(weighted, dirichlet_high, dirichlet_low)
        gather_relay(*block)

        gather_forward(*block)

        @pl.when(iteration == 0)
        def _():
            mix()

        gather_finish(*block)
        gathered = pieces[iteration].reshape(CG, RHS)
        picked = three(mixing[...], gathered, NN)
        values[...] = (values[...] + three(picked, basis[...], TN)) * weight[...]
        assemble(2 * iteration + 1, lambda: gather_leave(*block))
        adjoint[...] += values[...]
        return carry

    lax.fori_loop(0, ITERS, iterate, 0)
    gather_leave(inverse, inverse_sent, inverse_got)


def local(
    schur_block,
    dirichlet_inverse,
    coarse_basis,
    coarse_inverse,
    coarse_owner,
    face_count,
    face_rows,
    multiplicity,
    gradient,
    warm_start,
):
    my_owner = coarse_owner[0][:, None]
    inverse_block = jnp.concatenate(
        [coarse_inverse[0].T, jnp.broadcast_to(my_owner.astype(F32), (NCL, 128))], axis=1
    )
    live = jnp.arange(FMAX)[None, :] < face_count[0, 0][:, None]
    masked = jnp.where(live, face_rows[0, 0], NI).reshape(2, 2 * FMAX)
    weight = (1.0 / multiplicity[0, 0].astype(F32))[None, :]

    vmem = pl.BlockSpec(memory_space=pltpu.VMEM)
    out = pl.pallas_call(
        kernel,
        out_shape=jax.ShapeDtypeStruct((RHS, NI), F32),
        in_specs=[vmem] * 10,
        out_specs=vmem,
        scratch_shapes=[
            pltpu.VMEM((NI, NI), BF),
            pltpu.VMEM((NI, NI), BF),
            pltpu.VMEM((NI, NI), BF),
            pltpu.VMEM((NI, NI), BF),
            pltpu.VMEM((2, NI, 2 * FMAX), BF),
            pltpu.VMEM((2, 2 * FMAX, NI), BF),
            pltpu.VMEM((NCL, CG), F32),
            pltpu.VMEM((SUBS, NCL, CG + 128), F32),
            pltpu.VMEM((RHS, NI), F32),
            pltpu.VMEM((2 * RHS, NI), BF),
            pltpu.VMEM((4, RHS, FMAX), F32),
            pltpu.VMEM((2 * ITERS, 4, RHS, FMAX), F32),
            pltpu.VMEM((ITERS, SUBS, NCL, RHS), F32),
            pltpu.SemaphoreType.DMA((2 * ITERS, 4)),
            pltpu.SemaphoreType.DMA((2 * ITERS, 4)),
            pltpu.SemaphoreType.DMA((ITERS, SUBS)),
            pltpu.SemaphoreType.DMA((ITERS, SUBS)),
            pltpu.SemaphoreType.DMA((SUBS,)),
            pltpu.SemaphoreType.DMA((SUBS,)),
            pltpu.SemaphoreType.DMA,
        ],
        compiler_params=pltpu.CompilerParams(
            collective_id=0, has_side_effects=True, vmem_limit_bytes=63 * 1024 * 1024
        ),
    )(
        schur_block[0, 0], dirichlet_inverse[0, 0], coarse_basis[0, 0], inverse_block, my_owner,
        masked[:, None, :], masked[:, :, None], weight, gradient[0, 0], warm_start[0, 0],
    )
    return out[None, None]


def solution(mesh):
    in_specs = (
        P("grp", "sub", None, None),
        P("grp", "sub", None, None),
        P("grp", "sub", None, None),
        P("grp", None, "sub"),
        P("grp", "sub"),
        P("grp", "sub", None),
        P("grp", "sub", None, None),
        P("grp", "sub", None),
        P("grp", "sub", None, None),
        P("grp", "sub", None, None),
    )
    out_specs = P("grp", "sub", None, None)
    return jax.shard_map(local, mesh=mesh, in_specs=in_specs, out_specs=out_specs, check_vma=False)
```
